32 devices in a mesh: bins: 8 (over y, x, core), shells: 4 (over z).
Axes of the slice: x: 2, y: 2, z: 4, core: 2. Of those that a mesh axis runs over, the one named last changes fastest.
Arguments:
- map_tiles: bfloat16 [4, 4, 64, 8192], P('shells', None, None, 'bins'), may hold values from -3 to 3
- images: bfloat16 [2048, 4, 2, 8192], P('bins', 'shells'), may hold values from -6 to 6
- pose_bin: int32 [2048, 1], P('bins'), may hold values from 0 to 7; in each aligned block of 256 rows (0 to 255, 256 to 511, ...) at most 64 rows name the same one
- rot_index: int32 [2048], P('bins'), may hold values from 0 to 63
- shift_index: int32 [2048], P('bins'), may hold values from 0 to 48
- defocus_class: int32 [2048], P('bins'), may hold values from 0 to 15
- tile_slots: int32 [8, 4, 2], replicated, may hold values from -1 to 3, as said below
Outputs:
- map_gradient: float32 [4, 4, 64, 8192], P(None, None, 'shells', 'bins')
- particle_loss: float32 [2048, 4], P('bins', 'shells')
The draws below stay inside these ranges and needn't reach their ends.
Inputs may be any that keep to these rules, and one draw needn't show every extreme that they name: `pose_bin`: among the 256 particles of one device of bins, at most 64 share a pose bin, a bound that some block reaches of them. `tile_slots`: the tiles listed for one bin and band are distinct, slot 0 always holds a tile, and -1 is only followed by -1; some bin has all 2 slots filled in every band.
All inputs are finite; a program needn't handle non-finite values.
Results may differ from the reference program's by a relative error of at most 0.00081.
Values may be sent and summed in bfloat16 or wider, within the bound.
A program may use at most 256 MiB of HBM per device.

```python
import math
import jax
import jax.numpy as jnp
import numpy as np
from jax import lax

PLANES = 64
TILE_PIX = 4096
TB = 4
OCC = 2
ROTS = 64
SHIFTS = 49
DEFOCI = 16
PART_DEV = 256
PARTICLES = 2048
BINS = 8
BANDS = 4
CAP = 64


def draw_tile_slots(key, part):
    score_key = jax.random.fold_in(key, 11)
    count_key = jax.random.fold_in(key, 12)
    fullest_key = jax.random.fold_in(key, 13)
    scores = jax.random.randint(score_key, (BINS, BANDS, TB), 0, 1 << 20) * TB + jnp.arange(TB, dtype=jnp.int32)
    ordering = jnp.argsort(scores, axis=-1, stable=True).astype(jnp.int32)
    chosen = ordering[:, :, :OCC]
    counts = jax.random.randint(count_key, (BINS, BANDS), 1, OCC + 1)
    fullest = jax.random.randint(fullest_key, (), 0, BINS)
    counts = jnp.where(jnp.arange(BINS, dtype=jnp.int32)[:, None] == fullest, OCC, counts)
    slot_index = jnp.arange(OCC, dtype=jnp.int32)
    return jnp.where(slot_index[None, None, :] < counts[:, :, None], chosen, -1).astype(jnp.int32)


def set_ends(drawn, own_key, least, high):
    longest = drawn.shape.index(max(drawn.shape))
    spots = []
    for shift in (0, 1):
        where = [jax.random.randint(jax.random.fold_in(own_key, axis), (), 0, length) for axis, length in enumerate(drawn.shape)]
        where[longest] = (where[longest] + shift) % drawn.shape[longest]
        spots.append(tuple(where))
    return drawn.at[spots[0]].set(least).at[spots[1]].set(high)


def levels(rng, shape, pieces, low, top_value):
    def one(axis_at, parts):
        heights = jax.random.uniform(jax.random.fold_in(jax.random.fold_in(rng, 6), axis_at), (parts,), jnp.float32, low / len(pieces), top_value / len(pieces))
        return jnp.repeat(jnp.exp(heights), shape[axis_at] // parts).reshape((-1,) + (1,) * (len(shape) - axis_at - 1))

    gain = one(*pieces[0])
    for cut in pieces[1:]:
        gain = gain * one(*cut)
    return gain


def assign_block(own_key, own, number, rows, count, top, bound, skew):
    sequence = jax.random.permutation(own_key, count)
    packed, ordinary = portions_of(count, rows * top, bound, skew, True), portions_of(count, rows * top, bound, skew, False)
    places = jnp.arange(count)

    def named(lengths, turn):
        used = int((lengths > 0).sum())
        fixed = max(1, used // 4)
        moved = fixed + (places - fixed + turn * (used - fixed)) % max(1, count - fixed)
        return jnp.zeros((count,), jnp.int32).at[sequence[jnp.where(places < fixed, places, moved)]].set(jnp.asarray(lengths, jnp.int32))

    lengths = jnp.where(number % 4 == 0, named(packed, number // 4), named(ordinary, number - number // 4 - 1))
    mixed = jax.random.permutation(jax.random.fold_in(own, 3), count)
    source_of, taker = mixed[0:count // 2 * 2:2], mixed[1:count // 2 * 2:2]
    room = jnp.minimum(lengths[source_of] - 1, bound - lengths[taker]) // 2
    room = jnp.where((source_of == sequence[0]) | (taker == sequence[0]) | (lengths[taker] == 0), 0, jnp.maximum(room, 0))
    moved = jax.random.randint(jax.random.fold_in(own, 4), (count // 2,), 0, 1 << 20) % (room + 1)
    lengths = lengths.at[source_of].add(-moved).at[taker].add(moved)
    items = jnp.searchsorted(jnp.cumsum(lengths), jnp.arange(rows * top), side="right").astype(jnp.int32)
    listing = items.reshape(top, rows).T
    listing = listing[jax.random.permutation(jax.random.fold_in(own, 1), rows)]
    turn = jax.random.randint(jax.random.fold_in(own, 2), (rows, 1), 0, top)
    return jnp.take_along_axis(listing, (jnp.arange(top)[None, :] + turn) % top, axis=1)


def portions_of(number_of, total, reach, lean, full):
    weights = [(1 << 20) // math.isqrt(standing ** lean) + 1 for standing in range(1, number_of + 1)]
    largest = reach if full else min(reach, max(-(-total // number_of), total * weights[0] // sum(weights)))
    least = 1 if total - largest >= number_of - 1 else 0
    given, spare = [largest] + [least] * (number_of - 1), total - largest - least * (number_of - 1)
    while spare > 0:
        candidates = [i for i in range(1, number_of) if given[i] < largest] or [i for i in range(1, number_of) if given[i] < reach]
        whole, remaining = sum([weights[i] for i in candidates]), spare
        for i in candidates:
            more = min(reach - given[i], max(1, remaining * weights[i] // whole), spare)
            given[i] = given[i] + more
            spare = spare - more
    return np.array(given)


def centred(rng, dims, scale, limit, shards=(), kind=jnp.bfloat16):
    factor_of = levels(rng, dims, shards, -0.22, 0.18) if shards else 1.0
    values = jax.random.normal(rng, dims, jnp.float32) * scale * factor_of
    return jnp.minimum(jnp.maximum(values, -limit), limit).astype(kind)


def setup_inputs(seed: int = 0) -> dict:
    arg_keys = jax.random.split(jax.random.key(seed), 8)
    map_tiles = centred(arg_keys[0], (BANDS, TB, PLANES, 2 * TILE_PIX), 0.5, 3.0, ((0, 4), (3, 8)))
    images = centred(arg_keys[1], (PARTICLES, BANDS, OCC, 2 * TILE_PIX), 1.0, 6.0, ((0, 8), (1, 4)))
    pose_bin_keys = jax.random.split(jax.random.fold_in(arg_keys[2], 1), PARTICLES // PART_DEV)
    pose_bin_turns = jax.random.permutation(jax.random.fold_in(arg_keys[2], 3), PARTICLES // PART_DEV)
    pose_bin = jax.vmap(lambda own, number: assign_block(jax.random.fold_in(arg_keys[2], 2), own, number, PART_DEV, BINS, 1, CAP, 2))(pose_bin_keys, pose_bin_turns).reshape((PARTICLES, 1))
    rot_index = set_ends(jax.random.randint(arg_keys[3], (PARTICLES,), 0, ROTS), jax.random.fold_in(arg_keys[3], 1), 0, ROTS - 1).astype(jnp.int32)
    shift_index = set_ends(jax.random.randint(arg_keys[4], (PARTICLES,), 0, SHIFTS), jax.random.fold_in(arg_keys[4], 1), 0, SHIFTS - 1).astype(jnp.int32)
    defocus_class = set_ends(jax.random.randint(arg_keys[5], (PARTICLES,), 0, DEFOCI), jax.random.fold_in(arg_keys[5], 1), 0, DEFOCI - 1).astype(jnp.int32)
    tile_slots = draw_tile_slots(jax.random.fold_in(arg_keys[7], 71), 0)
    return {"map_tiles": map_tiles, "images": images, "pose_bin": pose_bin, "rot_index": rot_index, "shift_index": shift_index, "defocus_class": defocus_class, "tile_slots": tile_slots}


NOISE_PRECISION = 4.0
AMPLITUDE = 0.07

def plane_weights(rotation, bin_value, tile_safe, band_value, plane_count):
    pose_angle = 2.0 * math.pi / ROTS * rotation.astype(jnp.float32) + 0.7 * bin_value.astype(jnp.float32) + 1.3 * tile_safe.astype(jnp.float32) + 0.5 * band_value
    centre = 0.5 * (plane_count - 1) + 0.45 * plane_count * jnp.sin(pose_angle)
    offset = (jnp.arange(plane_count, dtype=jnp.float32) - centre[..., None]) / 1.5
    return jnp.exp(-0.5 * offset * offset).astype(jnp.bfloat16)

def pixel_terms(tile_safe, shifts, defocus, band_value, plane_count, band_count):
    cell_index = jnp.arange(plane_count * plane_count, dtype=jnp.int32)
    cell_row = cell_index // plane_count
    cell_col = cell_index % plane_count
    freq_x = (plane_count * (tile_safe % 2) - plane_count)[..., None] + cell_row
    freq_y = (plane_count * (tile_safe // 2 % 2) - plane_count)[..., None] + cell_col
    real_x = freq_x.astype(jnp.float32)
    real_y = freq_y.astype(jnp.float32)
    radial = (real_x * real_x + real_y * real_y) / (2.0 * plane_count) ** 2 + ((band_value + 1.0) / band_count) ** 2 / 4.0
    strength = 2.0 + 6.0 * defocus.astype(jnp.float32) / DEFOCI
    aberration = 8.0 * math.pi * strength[:, None, None] * radial
    contrast = -(math.sqrt(1.0 - AMPLITUDE * AMPLITUDE) * jnp.sin(aberration) + AMPLITUDE * jnp.cos(aberration))
    shift_x = (shifts % 7 - 3).astype(jnp.float32)[:, None, None]
    shift_y = (shifts // 7 - 3).astype(jnp.float32)[:, None, None]
    phase_angle = 2.0 * math.pi / (4.0 * plane_count) * (real_x * shift_x + real_y * shift_y)
    return (contrast, jnp.cos(phase_angle), jnp.sin(phase_angle))

def band_terms(slices, observed, occupied, contrast, cosine, sine_part, grad_scale):
    pixel_count = slices.shape[-1] // 2
    slot_count = slices.shape[1]
    real_slice = slices[..., :pixel_count]
    imag_slice = slices[..., pixel_count:]
    measured = observed.astype(jnp.float32)
    model_real = contrast * (cosine * real_slice + sine_part * imag_slice)
    model_imag = contrast * (cosine * imag_slice - sine_part * real_slice)
    resid_real = occupied[..., None] * (model_real - measured[..., :pixel_count])
    resid_imag = occupied[..., None] * (model_imag - measured[..., pixel_count:])
    band_loss = 2.0 * lax.optimization_barrier(jnp.sum(resid_real * resid_real + resid_imag * resid_imag, axis=(1, 2))) / (slot_count * 2 * pixel_count)
    grad_real = grad_scale * contrast * (cosine * resid_real - sine_part * resid_imag)
    grad_imag = grad_scale * contrast * (sine_part * resid_real + cosine * resid_imag)
    return (band_loss, jnp.concatenate([grad_real, grad_imag], axis=-1).astype(jnp.bfloat16))

def stack_weights(weights, tile_safe, tile_count):
    selector = (tile_safe[..., None] == jnp.arange(tile_count, dtype=jnp.int32)).astype(jnp.bfloat16)
    stacked = selector[..., None] * weights[..., None, :]
    return stacked.reshape(weights.shape[0] * weights.shape[1], tile_count * weights.shape[2])

def reference(map_tiles, images, pose_bin, rot_index, shift_index, defocus_class, tile_slots):
    pose_bins = pose_bin[:, 0]
    grad_scale = NOISE_PRECISION / math.sqrt(PARTICLES)
    block_count = PARTICLES // PART_DEV

    def one_band(band_index):
        band_value = band_index.astype(jnp.float32)
        flat_map = lax.dynamic_index_in_dim(map_tiles, band_index, 0, keepdims=False).reshape(TB * PLANES, 2 * TILE_PIX)
        band_slots = lax.dynamic_index_in_dim(tile_slots, band_index, 1, keepdims=False)
        band_images = lax.dynamic_index_in_dim(images, band_index, 1, keepdims=False)

        def one_block(running, block_index):
            first_row = (block_index * PART_DEV).astype(jnp.int32)
            block_bins = lax.dynamic_slice_in_dim(pose_bins, first_row, PART_DEV)
            rotation = lax.dynamic_slice_in_dim(rot_index, first_row, PART_DEV)
            shifts = lax.dynamic_slice_in_dim(shift_index, first_row, PART_DEV)
            defocus = lax.dynamic_slice_in_dim(defocus_class, first_row, PART_DEV)
            observed = lax.dynamic_slice_in_dim(band_images, first_row, PART_DEV)
            tile_ids = band_slots[block_bins]
            tile_safe = jnp.maximum(tile_ids, 0)
            occupied = (tile_ids >= 0).astype(jnp.float32)
            weights = plane_weights(rotation[:, None], block_bins[:, None], tile_safe, band_value, PLANES)
            stacked = stack_weights(weights, tile_safe, TB)
            slices = jnp.dot(stacked, flat_map, preferred_element_type=jnp.float32).reshape(PART_DEV, OCC, 2 * TILE_PIX)
            contrast, cosine, sine_part = pixel_terms(tile_safe, shifts, defocus, band_value, PLANES, BANDS)
            band_loss, slice_grad = band_terms(slices, observed, occupied, contrast, cosine, sine_part, grad_scale)
            running = running + jnp.dot(stacked.T, slice_grad.reshape(PART_DEV * OCC, 2 * TILE_PIX), preferred_element_type=jnp.float32)
            return (running, band_loss)
        start_grad = jnp.zeros((TB * PLANES, 2 * TILE_PIX), jnp.float32)
        band_grad, losses = lax.scan(one_block, start_grad, jnp.arange(block_count, dtype=jnp.int32))
        return (band_grad, losses.reshape(PARTICLES))
    band_grads, losses = lax.map(one_band, jnp.arange(BANDS, dtype=jnp.int32))
    return (band_grads.reshape(BANDS, TB, PLANES, 2 * TILE_PIX), jnp.transpose(losses))
```

```python
import math

import jax
import jax.numpy as jnp
from jax import lax
from jax.experimental import pallas as pl
from jax.experimental.pallas import tpu as pltpu
from jax.sharding import PartitionSpec as P

ROTS = 64
DEFOCI = 16
GRID = 7
NOISE_PRECISION = 4.0
AMPLITUDE = 0.07


def split_halves(table):
    rounded = lax.reduce_precision(table, 8, 7)
    high = rounded.astype(jnp.bfloat16)
    low = (table - rounded).astype(jnp.bfloat16)
    return jnp.concatenate([high, low], axis=0)


def contrast_table(band_value, plane_count, band_count):
    rows = jnp.arange(DEFOCI * 4, dtype=jnp.int32)[:, None]
    cell = jnp.arange(plane_count * plane_count, dtype=jnp.int32)[None, :]
    defocus = rows // 4
    real_x = (plane_count * (rows % 2) - plane_count + cell // plane_count).astype(jnp.float32)
    real_y = (plane_count * (rows // 2 % 2) - plane_count + cell % plane_count).astype(jnp.float32)
    radial = (real_x * real_x + real_y * real_y) / (2.0 * plane_count) ** 2 + (
        (band_value + 1.0) / band_count
    ) ** 2 / 4.0
    strength = 2.0 + 6.0 * defocus.astype(jnp.float32) / DEFOCI
    aberration = 8.0 * math.pi * strength * radial
    contrast = -(
        math.sqrt(1.0 - AMPLITUDE * AMPLITUDE) * jnp.sin(aberration)
        + AMPLITUDE * jnp.cos(aberration)
    )
    return split_halves(contrast)


def phase_table(plane_count, pad):
    rows = jnp.arange(GRID * GRID, dtype=jnp.int32)[:, None]
    cell = jnp.arange(plane_count * plane_count, dtype=jnp.int32)[None, :]
    turns = (cell // plane_count) * (rows % GRID - 3) + (cell % plane_count) * (rows // GRID - 3)
    angle = 2.0 * math.pi / (4.0 * plane_count) * turns.astype(jnp.float32)
    both = [split_halves(jnp.cos(angle)), split_halves(jnp.sin(angle))]
    used = 4 * GRID * GRID
    both.append(jnp.zeros((pad - used, cell.shape[1]), jnp.bfloat16))
    return jnp.concatenate(both, axis=0)


def selectors(shifts, defocus, tile_safe, pad):
    parity = tile_safe % 2 + 2 * (tile_safe // 2 % 2)
    pick = (
        (defocus * 4 + parity)[:, None]
        == (jnp.arange(2 * DEFOCI * 4, dtype=jnp.int32) % (DEFOCI * 4))[None, :]
    ).astype(jnp.bfloat16)
    sx = shifts % GRID - 3
    sy = shifts // GRID - 3
    quarter = ((1 - tile_safe % 2) * sx + (1 - tile_safe // 2 % 2) * sy + 64) % 4
    real_turn = jnp.where(quarter == 0, 1.0, jnp.where(quarter == 2, -1.0, 0.0))
    imag_turn = jnp.where(quarter == 1, -1.0, jnp.where(quarter == 3, 1.0, 0.0))
    column = jnp.arange(pad, dtype=jnp.int32)
    count = GRID * GRID
    match = (shifts[:, None] == (column % count)[None, :]).astype(jnp.float32)
    is_cos = (column < 2 * count).astype(jnp.float32)[None, :]
    is_sin = ((column >= 2 * count) & (column < 4 * count)).astype(jnp.float32)[None, :]
    cosine = match * (real_turn[:, None] * is_cos - imag_turn[:, None] * is_sin)
    sine = match * (imag_turn[:, None] * is_cos + real_turn[:, None] * is_sin)
    return pick, cosine.astype(jnp.bfloat16), sine.astype(jnp.bfloat16)


def row_weights(rotation, bins, tile_safe, occupied, band_value, tile_count, plane_count):
    pose_angle = (
        2.0 * math.pi / ROTS * rotation.astype(jnp.float32)
        + 0.7 * bins.astype(jnp.float32)
        + 1.3 * tile_safe.astype(jnp.float32)
        + 0.5 * band_value
    )
    centre = 0.5 * (plane_count - 1) + 0.45 * plane_count * jnp.sin(pose_angle)
    column = jnp.arange(tile_count * plane_count, dtype=jnp.int32)
    plane = (column % plane_count).astype(jnp.float32)
    offset = (plane[None, :] - centre[:, None]) / 1.5
    weights = jnp.exp(-0.5 * offset * offset)
    mine = (tile_safe[:, None] == (column // plane_count)[None, :]) & (occupied > 0)[:, None]
    return jnp.where(mine, weights, 0.0).astype(jnp.bfloat16)


def step_body(
    scale, w_ref, wt_ref, pick_ref, cos_ref, sin_ref, ctf_ref, phase_ref, map_ref, yr_ref, yi_ref,
    grad_ref, loss_ref,
):
    f32 = jnp.float32
    weights = w_ref[...]
    phases = phase_ref[...]
    part_a = jnp.dot(weights, map_ref[0, 0], preferred_element_type=f32)
    part_b = jnp.dot(weights, map_ref[1, 0], preferred_element_type=f32)
    contrast = jnp.dot(pick_ref[...], ctf_ref[...], preferred_element_type=f32)
    cosine = contrast * jnp.dot(cos_ref[...], phases, preferred_element_type=f32)
    sine = contrast * jnp.dot(sin_ref[...], phases, preferred_element_type=f32)
    resid_real = cosine * part_a + sine * part_b - yr_ref[...].astype(f32)
    resid_imag = cosine * part_b - sine * part_a - yi_ref[...].astype(f32)
    square = resid_real * resid_real + resid_imag * resid_imag
    total = square[:, :128]
    for at in range(128, square.shape[1], 128):
        total = total + square[:, at : at + 128]

    @pl.when(pl.program_id(0) == 0)
    def _():
        loss_ref[...] = jnp.zeros_like(loss_ref)

    loss_ref[...] += total
    cosine = scale * cosine
    sine = scale * sine
    grad_real = (cosine * resid_real - sine * resid_imag).astype(jnp.bfloat16)
    grad_imag = (sine * resid_real + cosine * resid_imag).astype(jnp.bfloat16)
    back = wt_ref[...]
    grad_ref[0, 0] = jnp.dot(back, grad_real, preferred_element_type=f32)
    grad_ref[1, 0] = jnp.dot(back, grad_imag, preferred_element_type=f32)


def local_step(scale, weights, pick, cosine, sine, ctf, phase, full_map, images):
    rows, depth = weights.shape
    halves, groups, _, cols = full_map.shape
    tile = min(256, cols)
    steps = groups * cols // tile
    per = cols // tile

    def whole(a):
        return pl.BlockSpec(a.shape, lambda g: (0,) * a.ndim)

    back = weights.T
    split = pl.BlockSpec((halves, 1, depth, tile), lambda g: (0, g // per, 0, g % per))
    return pl.pallas_call(
        lambda *refs: step_body(scale, *refs),
        grid=(steps,),
        in_specs=[
            whole(weights), whole(back), whole(pick), whole(cosine), whole(sine),
            pl.BlockSpec((ctf.shape[0], tile), lambda g: (0, g)),
            pl.BlockSpec((phase.shape[0], tile), lambda g: (0, g)),
            split,
            pl.BlockSpec((rows, tile), lambda g: (0, g)),
            pl.BlockSpec((rows, tile), lambda g: (0, steps + g)),
        ],
        out_specs=[split, pl.BlockSpec((rows, 128), lambda g: (0, 0))],
        out_shape=[
            jax.ShapeDtypeStruct(full_map.shape, jnp.float32),
            jax.ShapeDtypeStruct((rows, 128), jnp.float32),
        ],
        compiler_params=pltpu.CompilerParams(vmem_limit_bytes=48 * 2**20),
    )(weights, back, pick, cosine, sine, ctf, phase, full_map, images, images)


def on_device(map_tiles, images, pose_bin, rot_index, shift_index, defocus_class, tile_slots):
    band_index = lax.axis_index("shells")
    band_value = band_index.astype(jnp.float32)
    bin_count = lax.axis_size("bins")
    band_count = lax.axis_size("shells")
    part_count, _, slot_count, column_count = images.shape
    _, tile_count, plane_count, shard_cols = map_tiles.shape
    rows = part_count * slot_count
    depth = tile_count * plane_count
    grad_scale = NOISE_PRECISION / math.sqrt(part_count * bin_count)
    gathered = lax.all_gather(map_tiles.reshape(1, depth, shard_cols), "bins", axis=0, tiled=True)
    band_slots = lax.dynamic_index_in_dim(tile_slots, band_index, 1, keepdims=False)

    def per_row(values):
        return jnp.repeat(values, slot_count)

    bins = per_row(pose_bin[:, 0])
    slot = jnp.arange(rows, dtype=jnp.int32) % slot_count
    flat_slots = band_slots.reshape(-1)
    chosen = (bins * slot_count + slot)[:, None] == jnp.arange(flat_slots.shape[0])[None, :]
    tiles = jnp.sum(jnp.where(chosen, flat_slots[None, :], 0), axis=1)
    occupied = (tiles >= 0).astype(jnp.float32)
    tile_safe = jnp.maximum(tiles, 0)
    weights = row_weights(
        per_row(rot_index), bins, tile_safe, occupied, band_value, tile_count, plane_count
    )
    pad = 256
    pick, cosine, sine = selectors(per_row(shift_index), per_row(defocus_class), tile_safe, pad)
    ctf = contrast_table(band_value, plane_count, band_count)
    phase = phase_table(plane_count, pad)
    partial, losses = local_step(
        grad_scale, weights, pick, cosine, sine, ctf, phase,
        gathered.reshape(2, bin_count // 2, depth, shard_cols),
        images.reshape(rows, column_count),
    )
    band_loss = (
        2.0
        * jnp.sum((losses * occupied[:, None]).reshape(part_count, slot_count * 128), axis=1)
        / (slot_count * column_count)
    )
    grad_shard = lax.psum_scatter(
        partial.reshape(bin_count, depth, shard_cols), "bins", scatter_dimension=0, tiled=True
    )
    gradient = lax.all_to_all(
        grad_shard.reshape(1, tile_count, plane_count, shard_cols),
        "shells",
        split_axis=2,
        concat_axis=0,
        tiled=True,
    )
    return (gradient, band_loss[:, None])


def solution(mesh):
    return jax.shard_map(
        on_device,
        mesh=mesh,
        in_specs=(
            P("shells", None, None, "bins"),
            P("bins", "shells", None, None),
            P("bins", None),
            P("bins"),
            P("bins"),
            P("bins"),
            P(),
        ),
        out_specs=(P(None, None, "shells", "bins"), P("bins", "shells")),
        check_vma=False,
    )
```

```python
import math

import jax
import jax.numpy as jnp
from jax import lax
from jax.experimental import pallas as pl
from jax.experimental.pallas import tpu as pltpu
from jax.sharding import PartitionSpec as P

ROTS = 64
DEFOCI = 16
GRID = 7
NOISE_PRECISION = 4.0
AMPLITUDE = 0.07


def split_halves(table):
    rounded = lax.reduce_precision(table, 8, 7)
    high = rounded.astype(jnp.bfloat16)
    low = (table - rounded).astype(jnp.bfloat16)
    return jnp.concatenate([high, low], axis=0)


def contrast_table(band_value, plane_count, band_count):
    rows = jnp.arange(DEFOCI * 4, dtype=jnp.int32)[:, None]
    cell = jnp.arange(plane_count * plane_count, dtype=jnp.int32)[None, :]
    defocus = rows // 4
    real_x = (plane_count * (rows % 2) - plane_count + cell // plane_count).astype(jnp.float32)
    real_y = (plane_count * (rows // 2 % 2) - plane_count + cell % plane_count).astype(jnp.float32)
    radial = (real_x * real_x + real_y * real_y) / (2.0 * plane_count) ** 2 + (
        (band_value + 1.0) / band_count
    ) ** 2 / 4.0
    strength = 2.0 + 6.0 * defocus.astype(jnp.float32) / DEFOCI
    aberration = 8.0 * math.pi * strength * radial
    contrast = -(
        math.sqrt(1.0 - AMPLITUDE * AMPLITUDE) * jnp.sin(aberration)
        + AMPLITUDE * jnp.cos(aberration)
    )
    return split_halves(contrast)


def phase_table(plane_count, pad):
    steps = (jnp.arange(8, dtype=jnp.int32) - 3)[:, None]
    cell = jnp.arange(plane_count * plane_count, dtype=jnp.int32)[None, :]
    unit = 2.0 * math.pi / (4.0 * plane_count)
    along_x = unit * ((cell // plane_count) * steps).astype(jnp.float32)
    along_y = unit * ((cell % plane_count) * steps).astype(jnp.float32)
    cos_x, sin_x, cos_y, sin_y = lax.optimization_barrier(
        (jnp.cos(along_x), jnp.sin(along_x), jnp.cos(along_y[:GRID]), jnp.sin(along_y[:GRID]))
    )
    cosine = cos_y[:, None] * cos_x[None] - sin_y[:, None] * sin_x[None]
    sine = sin_y[:, None] * cos_x[None] + cos_y[:, None] * sin_x[None]
    both = [split_halves(t.reshape(GRID * 8, cell.shape[1])) for t in (cosine, sine)]
    both.append(jnp.zeros((pad - 4 * GRID * 8, cell.shape[1]), jnp.bfloat16))
    return jnp.concatenate(both, axis=0)


def selectors(shifts, defocus, tile_safe, pad):
    parity = tile_safe % 2 + 2 * (tile_safe // 2 % 2)
    pick = (
        (defocus * 4 + parity)[:, None]
        == (jnp.arange(2 * DEFOCI * 4, dtype=jnp.int32) % (DEFOCI * 4))[None, :]
    ).astype(jnp.bfloat16)
    sx = shifts % GRID - 3
    sy = shifts // GRID - 3
    quarter = ((1 - tile_safe % 2) * sx + (1 - tile_safe // 2 % 2) * sy + 64) % 4
    real_turn = jnp.where(quarter == 0, 1.0, jnp.where(quarter == 2, -1.0, 0.0))
    imag_turn = jnp.where(quarter == 1, -1.0, jnp.where(quarter == 3, 1.0, 0.0))
    column = jnp.arange(pad, dtype=jnp.int32)
    count = GRID * 8
    match = ((shifts + shifts // GRID)[:, None] == (column % count)[None, :]).astype(jnp.float32)
    is_cos = (column < 2 * count).astype(jnp.float32)[None, :]
    is_sin = ((column >= 2 * count) & (column < 4 * count)).astype(jnp.float32)[None, :]
    cosine = match * (real_turn[:, None] * is_cos - imag_turn[:, None] * is_sin)
    sine = match * (imag_turn[:, None] * is_cos + real_turn[:, None] * is_sin)
    return pick, cosine.astype(jnp.bfloat16), sine.astype(jnp.bfloat16)


def row_weights(rotation, bins, tile_safe, occupied, band_value, tile_count, plane_count):
    pose_angle = (
        2.0 * math.pi / ROTS * rotation.astype(jnp.float32)
        + 0.7 * bins.astype(jnp.float32)
        + 1.3 * tile_safe.astype(jnp.float32)
        + 0.5 * band_value
    )
    centre = 0.5 * (plane_count - 1) + 0.45 * plane_count * jnp.sin(pose_angle)
    column = jnp.arange(tile_count * plane_count, dtype=jnp.int32)
    plane = (column % plane_count).astype(jnp.float32)
    offset = (plane[None, :] - centre[:, None]) / 1.5
    weights = jnp.exp(-0.5 * offset * offset)
    mine = (tile_safe[:, None] == (column // plane_count)[None, :]) & (occupied > 0)[:, None]
    return jnp.where(mine, weights, 0.0).astype(jnp.bfloat16)


def fused_step(
    scale, bands, w_ref, wt_ref, pick_ref, cos_ref, sin_ref, ctf_ref, phase_ref, map_ref, img_ref,
    out_ref, loss_ref,
    mine, theirs, pair_in, chip_in, final,
    pair_send, pair_recv, chip_send, chip_recv, band_send, band_recv,
):
    f32 = jnp.float32
    _, groups, depth, cols = map_ref.shape
    rounds = groups // 2
    chips = groups
    tiles, planes = out_ref.shape[1], depth // out_ref.shape[1]
    part = out_ref.shape[2]
    me = lax.axis_index("bins")
    chip, core = me // 2, me % 2
    band = lax.axis_index("shells")
    tile = min(256, cols)
    mesh_ids = pl.DeviceIdType.MESH

    partner = {"bins": chip * 2 + (1 - core)}
    peers = [{"bins": (chip + r) % chips * 2 + core} for r in range(1, chips)]
    stack = [{"shells": (band + q) % bands} for q in range(1, bands)]
    barrier = pltpu.get_barrier_semaphore()
    for other in [partner] + peers + stack:
        pl.semaphore_signal(barrier, inc=1, device_id=other, device_id_type=mesh_ids)
    pl.semaphore_wait(barrier, 1 + len(peers) + len(stack))
    loss_ref[...] = jnp.zeros_like(loss_ref)

    def compute(group, target):
        def columns(at, carry):
            inside = pl.ds(pl.multiple_of(at * tile, tile), tile)
            base = group * cols + at * tile
            cells = pl.ds(pl.multiple_of(base, tile), tile)
            imag_cells = pl.ds(pl.multiple_of(groups * cols + base, tile), tile)
            weights = w_ref[...]
            phases = phase_ref[:, cells]
            part_a = jnp.dot(weights, map_ref[0, group, :, inside], preferred_element_type=f32)
            part_b = jnp.dot(weights, map_ref[1, group, :, inside], preferred_element_type=f32)
            contrast = jnp.dot(pick_ref[...], ctf_ref[:, cells], preferred_element_type=f32)
            cosine = contrast * jnp.dot(cos_ref[...], phases, preferred_element_type=f32)
            sine = contrast * jnp.dot(sin_ref[...], phases, preferred_element_type=f32)
            resid_real = cosine * part_a + sine * part_b - img_ref[:, cells].astype(f32)
            resid_imag = cosine * part_b - sine * part_a - img_ref[:, imag_cells].astype(f32)
            square = resid_real * resid_real + resid_imag * resid_imag
            total = square[:, :128]
            for lane in range(128, tile, 128):
                total = total + square[:, lane : lane + 128]
            loss_ref[...] += total
            cosine = scale * cosine
            sine = scale * sine
            grad_real = (cosine * resid_real - sine * resid_imag).astype(jnp.bfloat16)
            grad_imag = (sine * resid_real + cosine * resid_imag).astype(jnp.bfloat16)
            back = wt_ref[...]
            target[0, :, inside] = jnp.dot(back, grad_real, preferred_element_type=f32)
            target[1, :, inside] = jnp.dot(back, grad_imag, preferred_element_type=f32)
            return carry

        lax.fori_loop(0, cols // tile, columns, 0)

    def to_partner(turn):
        return pltpu.make_async_remote_copy(
            src_ref=theirs.at[turn], dst_ref=pair_in.at[turn],
            send_sem=pair_send.at[turn], recv_sem=pair_recv.at[turn],
            device_id=partner, device_id_type=mesh_ids,
        )

    def rows_of(t):
        return pl.ds(t * planes, planes)

    def to_chip(turn, hop, t):
        half = (chip + hop) % chips // rounds
        return pltpu.make_async_remote_copy(
            src_ref=mine.at[turn, half, rows_of(t)], dst_ref=chip_in.at[hop - 1, rows_of(t)],
            send_sem=chip_send.at[hop - 1, t], recv_sem=chip_recv.at[hop - 1, t],
            device_id=peers[hop - 1], device_id_type=mesh_ids,
        )

    def to_band(hop, t):
        there = (band + hop) % bands
        return pltpu.make_async_remote_copy(
            src_ref=final.at[pl.ds(pl.multiple_of(t * planes + there * part, 8), part)],
            dst_ref=out_ref.at[band, t],
            send_sem=band_send.at[hop - 1, t], recv_sem=band_recv.at[hop - 1, t],
            device_id=stack[hop - 1], device_id_type=mesh_ids,
        )

    for turn in range(rounds):
        pair = (chip + turn + 1) % rounds
        compute(pair * 2 + (1 - core), theirs.at[turn])
        to_partner(turn).start()
        compute(pair * 2 + core, mine.at[turn])
        to_partner(turn).wait_recv()
        hops = [(turn + 1) % chips, (turn + 1 + rounds) % chips]
        for t in range(tiles):
            for half in range(2):
                mine[turn, half, rows_of(t)] += pair_in[turn, half, rows_of(t)]
            for hop in hops:
                if hop:
                    to_chip(turn, hop, t).start()

    own = chip // rounds
    for t in range(tiles):
        total = mine[rounds - 1, own, rows_of(t)]
        for hop in range(1, chips):
            to_chip((hop - 1) % rounds, hop, t).wait_recv()
            total = total + chip_in[hop - 1, rows_of(t)]
        final[rows_of(t)] = total
        for hop in range(1, bands):
            to_band(hop, t).start()
        out_ref[band, t] = final[pl.ds(pl.multiple_of(t * planes + band * part, 8), part)]

    for turn in range(rounds):
        to_partner(turn).wait_send()
    for t in range(tiles):
        for hop in range(1, chips):
            to_chip((hop - 1) % rounds, hop, t).wait_send()
        for hop in range(1, bands):
            to_band(hop, t).wait()


def local_step(scale, bands, tiles, weights, pick, cosine, sine, ctf, phase, full_map, images):
    rows, depth = weights.shape
    _, groups, _, cols = full_map.shape
    rounds, part = groups // 2, depth // tiles // bands
    f32 = jnp.float32
    vmem = pl.BlockSpec(memory_space=pltpu.VMEM)
    dma = pltpu.SemaphoreType.DMA
    return pl.pallas_call(
        lambda *refs: fused_step(scale, bands, *refs),
        in_specs=[vmem] * 9,
        out_specs=[vmem] * 2,
        out_shape=[
            jax.ShapeDtypeStruct((bands, tiles, part, cols), f32),
            jax.ShapeDtypeStruct((rows, 128), f32),
        ],
        scratch_shapes=[
            pltpu.VMEM((rounds, 2, depth, cols), f32),
            pltpu.VMEM((rounds, 2, depth, cols), f32),
            pltpu.VMEM((rounds, 2, depth, cols), f32),
            pltpu.VMEM((groups - 1, depth, cols), f32),
            pltpu.VMEM((depth, cols), f32),
            dma((rounds,)),
            dma((rounds,)),
            dma((groups - 1, tiles)),
            dma((groups - 1, tiles)),
            dma((bands - 1, tiles)),
            dma((bands - 1, tiles)),
        ],
        compiler_params=pltpu.CompilerParams(
            vmem_limit_bytes=62 * 2**20, collective_id=0, has_side_effects=True
        ),
    )(weights, weights.T, pick, cosine, sine, ctf, phase, full_map, images)


def on_device(map_tiles, images, pose_bin, rot_index, shift_index, defocus_class, tile_slots):
    band_index = lax.axis_index("shells")
    band_value = band_index.astype(jnp.float32)
    bin_count = lax.axis_size("bins")
    band_count = lax.axis_size("shells")
    part_count, _, slot_count, column_count = images.shape
    _, tile_count, plane_count, shard_cols = map_tiles.shape
    rows = part_count * slot_count
    depth = tile_count * plane_count
    grad_scale = NOISE_PRECISION / math.sqrt(part_count * bin_count)
    gathered = lax.all_gather(map_tiles.reshape(1, depth, shard_cols), "bins", axis=0, tiled=True)
    band_slots = lax.dynamic_index_in_dim(tile_slots, band_index, 1, keepdims=False)

    def per_row(values):
        return jnp.repeat(values, slot_count)

    bins = per_row(pose_bin[:, 0])
    slot = jnp.arange(rows, dtype=jnp.int32) % slot_count
    flat_slots = band_slots.reshape(-1)
    chosen = (bins * slot_count + slot)[:, None] == jnp.arange(flat_slots.shape[0])[None, :]
    tiles = jnp.sum(jnp.where(chosen, flat_slots[None, :], 0), axis=1)
    occupied = (tiles >= 0).astype(jnp.float32)
    tile_safe = jnp.maximum(tiles, 0)
    weights = row_weights(
        per_row(rot_index), bins, tile_safe, occupied, band_value, tile_count, plane_count
    )
    pad = 256
    pick, cosine, sine = selectors(per_row(shift_index), per_row(defocus_class), tile_safe, pad)
    ctf = contrast_table(band_value, plane_count, band_count)
    phase = phase_table(plane_count, pad)
    gradient, losses = local_step(
        grad_scale, band_count, tile_count, weights, pick, cosine, sine, ctf, phase,
        gathered.reshape(2, bin_count // 2, depth, shard_cols),
        images.reshape(rows, column_count),
    )
    band_loss = (
        2.0
        * jnp.sum((losses * occupied[:, None]).reshape(part_count, slot_count * 128), axis=1)
        / (slot_count * column_count)
    )
    return (gradient, band_loss[:, None])


def solution(mesh):
    return jax.shard_map(
        on_device,
        mesh=mesh,
        in_specs=(
            P("shells", None, None, "bins"),
            P("bins", "shells", None, None),
            P("bins", None),
            P("bins"),
            P("bins"),
            P("bins"),
            P(),
        ),
        out_specs=(P(None, None, "shells", "bins"), P("bins", "shells")),
        check_vma=False,
    )
```

```python
import math

import jax
import jax.numpy as jnp
from jax import lax
from jax.experimental import pallas as pl
from jax.experimental.pallas import tpu as pltpu
from jax.sharding import PartitionSpec as P

ROTS = 64
DEFOCI = 16
GRID = 7
NOISE_PRECISION = 4.0
AMPLITUDE = 0.07


def split_halves(table):
    rounded = lax.reduce_precision(table, 8, 7)
    high = rounded.astype(jnp.bfloat16)
    low = (table - rounded).astype(jnp.bfloat16)
    return jnp.concatenate([high, low], axis=0)


def contrast_table(band_value, plane_count, band_count):
    rows = jnp.arange(DEFOCI * 4, dtype=jnp.int32)[:, None]
    cell = jnp.arange(plane_count * plane_count, dtype=jnp.int32)[None, :]
    defocus = rows // 4
    real_x = (plane_count * (rows % 2) - plane_count + cell // plane_count).astype(jnp.float32)
    real_y = (plane_count * (rows // 2 % 2) - plane_count + cell % plane_count).astype(jnp.float32)
    radial = (real_x * real_x + real_y * real_y) / (2.0 * plane_count) ** 2 + (
        (band_value + 1.0) / band_count
    ) ** 2 / 4.0
    strength = 2.0 + 6.0 * defocus.astype(jnp.float32) / DEFOCI
    aberration = 8.0 * math.pi * strength * radial
    contrast = -(
        math.sqrt(1.0 - AMPLITUDE * AMPLITUDE) * jnp.sin(aberration)
        + AMPLITUDE * jnp.cos(aberration)
    )
    return split_halves(contrast)


def phase_table(plane_count, pad):
    steps = (jnp.arange(8, dtype=jnp.int32) - 3)[:, None]
    cell = jnp.arange(plane_count * plane_count, dtype=jnp.int32)[None, :]
    unit = 2.0 * math.pi / (4.0 * plane_count)
    along_x = unit * ((cell // plane_count) * steps).astype(jnp.float32)
    along_y = unit * ((cell % plane_count) * steps).astype(jnp.float32)
    cos_x, sin_x, cos_y, sin_y = lax.optimization_barrier(
        (jnp.cos(along_x), jnp.sin(along_x), jnp.cos(along_y[:GRID]), jnp.sin(along_y[:GRID]))
    )
    cosine = cos_y[:, None] * cos_x[None] - sin_y[:, None] * sin_x[None]
    sine = sin_y[:, None] * cos_x[None] + cos_y[:, None] * sin_x[None]
    both = [split_halves(t.reshape(GRID * 8, cell.shape[1])) for t in (cosine, sine)]
    both.append(jnp.zeros((pad - 4 * GRID * 8, cell.shape[1]), jnp.bfloat16))
    return jnp.concatenate(both, axis=0)


def selectors(shifts, defocus, tile_safe, pad):
    parity = tile_safe % 2 + 2 * (tile_safe // 2 % 2)
    pick = (
        (defocus * 4 + parity)[:, None]
        == (jnp.arange(2 * DEFOCI * 4, dtype=jnp.int32) % (DEFOCI * 4))[None, :]
    ).astype(jnp.bfloat16)
    sx = shifts % GRID - 3
    sy = shifts // GRID - 3
    quarter = ((1 - tile_safe % 2) * sx + (1 - tile_safe // 2 % 2) * sy + 64) % 4
    real_turn = jnp.where(quarter == 0, 1.0, jnp.where(quarter == 2, -1.0, 0.0))
    imag_turn = jnp.where(quarter == 1, -1.0, jnp.where(quarter == 3, 1.0, 0.0))
    column = jnp.arange(pad, dtype=jnp.int32)
    count = GRID * 8
    match = ((shifts + shifts // GRID)[:, None] == (column % count)[None, :]).astype(jnp.float32)
    is_cos = (column < 2 * count).astype(jnp.float32)[None, :]
    is_sin = ((column >= 2 * count) & (column < 4 * count)).astype(jnp.float32)[None, :]
    cosine = match * (real_turn[:, None] * is_cos - imag_turn[:, None] * is_sin)
    sine = match * (imag_turn[:, None] * is_cos + real_turn[:, None] * is_sin)
    return pick, cosine.astype(jnp.bfloat16), sine.astype(jnp.bfloat16)


def row_weights(rotation, bins, tile_safe, occupied, band_value, tile_count, plane_count):
    pose_angle = (
        2.0 * math.pi / ROTS * rotation.astype(jnp.float32)
        + 0.7 * bins.astype(jnp.float32)
        + 1.3 * tile_safe.astype(jnp.float32)
        + 0.5 * band_value
    )
    centre = 0.5 * (plane_count - 1) + 0.45 * plane_count * jnp.sin(pose_angle)
    column = jnp.arange(tile_count * plane_count, dtype=jnp.int32)
    plane = (column % plane_count).astype(jnp.float32)
    offset = (plane[None, :] - centre[:, None]) / 1.5
    weights = jnp.exp(-0.5 * offset * offset)
    mine = (tile_safe[:, None] == (column // plane_count)[None, :]) & (occupied > 0)[:, None]
    return jnp.where(mine, weights, 0.0).astype(jnp.bfloat16)


def fused_step(
    scale, bands, w_ref, wt_ref, pick_ref, cos_ref, sin_ref, ctf_ref, phase_ref, shard_ref, img_ref,
    out_ref, loss_ref,
    map_ref, mine, theirs, pair_in, chip_in, final,
    own_sem, map_send, map_recv, share_send, share_recv,
    pair_send, pair_recv, chip_send, chip_recv, band_send, band_recv,
):
    f32 = jnp.float32
    _, groups, depth, cols = map_ref.shape
    rounds = groups // 2
    chips = groups
    tiles, planes = out_ref.shape[1], depth // out_ref.shape[1]
    part = out_ref.shape[2]
    me = lax.axis_index("bins")
    chip, core = me // 2, me % 2
    band = lax.axis_index("shells")
    tile = min(256, cols)
    mesh_ids = pl.DeviceIdType.MESH

    partner = {"bins": chip * 2 + (1 - core)}
    peers = [{"bins": (chip + r) % chips * 2 + core} for r in range(1, chips)]
    stack = [{"shells": (band + q) % bands} for q in range(1, bands)]
    barrier = pltpu.get_barrier_semaphore()
    for other in [partner] + peers + stack:
        pl.semaphore_signal(barrier, inc=1, device_id=other, device_id_type=mesh_ids)
    pl.semaphore_wait(barrier, 1 + len(peers) + len(stack))

    def block_of(device):
        return map_ref.at[device // groups, device % groups]

    def to_map(hop):
        return pltpu.make_async_remote_copy(
            src_ref=shard_ref, dst_ref=block_of(me),
            send_sem=map_send.at[hop - 1], recv_sem=map_recv.at[hop - 1],
            device_id=peers[hop - 1], device_id_type=mesh_ids,
        )

    def to_share(hop):
        source = (chip - hop + chips) % chips * 2 + core
        return pltpu.make_async_remote_copy(
            src_ref=block_of(source) if hop else shard_ref, dst_ref=block_of(source),
            send_sem=share_send.at[hop], recv_sem=share_recv.at[hop],
            device_id=partner, device_id_type=mesh_ids,
        )

    def hops_of(turn):
        return [(turn + 1) % chips, (turn + 1 + rounds) % chips]

    for turn in range(rounds):
        for hop in hops_of(turn):
            if hop:
                to_map(hop).start()
    to_share(0).start()
    keep = pltpu.make_async_copy(shard_ref, block_of(me), own_sem)
    keep.start()
    loss_ref[...] = jnp.zeros_like(loss_ref)

    def observed(start):
        lanes = [img_ref[start // 128 + at].astype(f32) for at in range(tile // 128)]
        return jnp.concatenate(lanes, axis=1)

    def compute(group, target):
        def columns(at, carry):
            inside = pl.ds(pl.multiple_of(at * tile, tile), tile)
            base = group * cols + at * tile
            cells = pl.ds(pl.multiple_of(base, tile), tile)
            weights = w_ref[...]
            phases = phase_ref[:, cells]
            part_a = jnp.dot(weights, map_ref[0, group, :, inside], preferred_element_type=f32)
            part_b = jnp.dot(weights, map_ref[1, group, :, inside], preferred_element_type=f32)
            contrast = jnp.dot(pick_ref[...], ctf_ref[:, cells], preferred_element_type=f32)
            cosine = contrast * jnp.dot(cos_ref[...], phases, preferred_element_type=f32)
            sine = contrast * jnp.dot(sin_ref[...], phases, preferred_element_type=f32)
            resid_real = cosine * part_a + sine * part_b - observed(base)
            resid_imag = cosine * part_b - sine * part_a - observed(groups * cols + base)
            square = resid_real * resid_real + resid_imag * resid_imag
            total = square[:, :128]
            for lane in range(128, tile, 128):
                total = total + square[:, lane : lane + 128]
            loss_ref[...] += total
            cosine = scale * cosine
            sine = scale * sine
            grad_real = (cosine * resid_real - sine * resid_imag).astype(jnp.bfloat16)
            grad_imag = (sine * resid_real + cosine * resid_imag).astype(jnp.bfloat16)
            back = wt_ref[...]
            target[0, :, inside] = jnp.dot(back, grad_real, preferred_element_type=f32)
            target[1, :, inside] = jnp.dot(back, grad_imag, preferred_element_type=f32)
            return carry

        lax.fori_loop(0, cols // tile, columns, 0)

    def to_partner(turn):
        return pltpu.make_async_remote_copy(
            src_ref=theirs.at[turn], dst_ref=pair_in.at[turn],
            send_sem=pair_send.at[turn], recv_sem=pair_recv.at[turn],
            device_id=partner, device_id_type=mesh_ids,
        )

    def rows_of(t):
        return pl.ds(t * planes, planes)

    def to_chip(turn, hop, t):
        half = (chip + hop) % chips // rounds
        return pltpu.make_async_remote_copy(
            src_ref=mine.at[turn, half, rows_of(t)], dst_ref=chip_in.at[hop - 1, rows_of(t)],
            send_sem=chip_send.at[hop - 1, t], recv_sem=chip_recv.at[hop - 1, t],
            device_id=peers[hop - 1], device_id_type=mesh_ids,
        )

    def to_band(hop, t):
        there = (band + hop) % bands
        return pltpu.make_async_remote_copy(
            src_ref=final.at[pl.ds(pl.multiple_of(t * planes + there * part, 8), part)],
            dst_ref=out_ref.at[band, t],
            send_sem=band_send.at[hop - 1, t], recv_sem=band_recv.at[hop - 1, t],
            device_id=stack[hop - 1], device_id_type=mesh_ids,
        )

    def combine(turn):
        to_partner(turn).wait_recv()
        for t in range(tiles):
            for half in range(2):
                mine[turn, half, rows_of(t)] += pair_in[turn, half, rows_of(t)]
            for hop in hops_of(turn):
                if hop:
                    to_chip(turn, hop, t).start()

    for turn in range(rounds):
        pair = (chip + turn + 1) % rounds
        for hop in hops_of(turn):
            if hop:
                to_map(chips - hop).wait_recv()
                to_share(chips - hop).start()
            else:
                keep.wait()
        compute(pair * 2 + core, mine.at[turn])
        if turn:
            combine(turn - 1)
        for hop in hops_of(turn):
            to_share((chips - hop) % chips).wait_recv()
        compute(pair * 2 + (1 - core), theirs.at[turn])
        to_partner(turn).start()
    combine(rounds - 1)

    own = chip // rounds
    for t in range(tiles):
        total = mine[rounds - 1, own, rows_of(t)]
        for hop in range(1, chips):
            to_chip((hop - 1) % rounds, hop, t).wait_recv()
            total = total + chip_in[hop - 1, rows_of(t)]
        final[rows_of(t)] = total
        for hop in range(1, bands):
            to_band(hop, t).start()
        out_ref[band, t] = final[pl.ds(pl.multiple_of(t * planes + band * part, 8), part)]

    to_share(0).wait_send()
    for hop in range(1, chips):
        to_map(hop).wait_send()
        to_share(hop).wait_send()
    for turn in range(rounds):
        to_partner(turn).wait_send()
    for t in range(tiles):
        for hop in range(1, chips):
            to_chip((hop - 1) % rounds, hop, t).wait_send()
        for hop in range(1, bands):
            to_band(hop, t).wait()


def local_step(scale, bands, tiles, weights, pick, cosine, sine, ctf, phase, shard, bins, images):
    rows, depth = weights.shape
    groups, cols = bins // 2, shard.shape[1]
    rounds, part = groups // 2, depth // tiles // bands
    f32 = jnp.float32
    vmem = pl.BlockSpec(memory_space=pltpu.VMEM)
    dma = pltpu.SemaphoreType.DMA
    return pl.pallas_call(
        lambda *refs: fused_step(scale, bands, *refs),
        in_specs=[vmem] * 9,
        out_specs=[vmem] * 2,
        out_shape=[
            jax.ShapeDtypeStruct((bands, tiles, part, cols), f32),
            jax.ShapeDtypeStruct((rows, 128), f32),
        ],
        scratch_shapes=[
            pltpu.VMEM((2, groups, depth, cols), jnp.bfloat16),
            pltpu.VMEM((rounds, 2, depth, cols), f32),
            pltpu.VMEM((rounds, 2, depth, cols), f32),
            pltpu.VMEM((rounds, 2, depth, cols), f32),
            pltpu.VMEM((groups - 1, depth, cols), f32),
            pltpu.VMEM((depth, cols), f32),
            dma,
            dma((groups - 1,)),
            dma((groups - 1,)),
            dma((groups,)),
            dma((groups,)),
            dma((rounds,)),
            dma((rounds,)),
            dma((groups - 1, tiles)),
            dma((groups - 1, tiles)),
            dma((bands - 1, tiles)),
            dma((bands - 1, tiles)),
        ],
        compiler_params=pltpu.CompilerParams(
            vmem_limit_bytes=62 * 2**20, collective_id=0, has_side_effects=True
        ),
    )(weights, weights.T, pick, cosine, sine, ctf, phase, shard, images)


def on_device(map_tiles, images, pose_bin, rot_index, shift_index, defocus_class, tile_slots):
    band_index = lax.axis_index("shells")
    band_value = band_index.astype(jnp.float32)
    bin_count = lax.axis_size("bins")
    band_count = lax.axis_size("shells")
    part_count, _, slot_count, column_count = images.shape
    _, tile_count, plane_count, shard_cols = map_tiles.shape
    rows = part_count * slot_count
    depth = tile_count * plane_count
    grad_scale = NOISE_PRECISION / math.sqrt(part_count * bin_count)
    lane_images = (
        images.reshape(part_count, slot_count, column_count // 128, 128)
        .transpose(2, 0, 1, 3)
        .reshape(column_count // 128, rows, 128)
    )
    band_slots = lax.dynamic_index_in_dim(tile_slots, band_index, 1, keepdims=False)

    def per_row(values):
        return jnp.repeat(values, slot_count)

    bins = per_row(pose_bin[:, 0])
    slot = jnp.arange(rows, dtype=jnp.int32) % slot_count
    flat_slots = band_slots.reshape(-1)
    chosen = (bins * slot_count + slot)[:, None] == jnp.arange(flat_slots.shape[0])[None, :]
    tiles = jnp.sum(jnp.where(chosen, flat_slots[None, :], 0), axis=1)
    occupied = (tiles >= 0).astype(jnp.float32)
    tile_safe = jnp.maximum(tiles, 0)
    weights = row_weights(
        per_row(rot_index), bins, tile_safe, occupied, band_value, tile_count, plane_count
    )
    pad = 256
    pick, cosine, sine = selectors(per_row(shift_index), per_row(defocus_class), tile_safe, pad)
    ctf = contrast_table(band_value, plane_count, band_count)
    phase = phase_table(plane_count, pad)
    gradient, losses = local_step(
        grad_scale, band_count, tile_count, weights, pick, cosine, sine, ctf, phase,
        map_tiles.reshape(depth, shard_cols), bin_count, lane_images,
    )
    band_loss = (
        2.0
        * jnp.sum((losses * occupied[:, None]).reshape(part_count, slot_count * 128), axis=1)
        / (slot_count * column_count)
    )
    return (gradient, band_loss[:, None])


def solution(mesh):
    return jax.shard_map(
        on_device,
        mesh=mesh,
        in_specs=(
            P("shells", None, None, "bins"),
            P("bins", "shells", None, None),
            P("bins", None),
            P("bins"),
            P("bins"),
            P("bins"),
            P(),
        ),
        out_specs=(P(None, None, "shells", "bins"), P("bins", "shells")),
        check_vma=False,
    )
```

```python
import math

import jax
import jax.numpy as jnp
from jax import lax
from jax.experimental import pallas as pl
from jax.experimental.pallas import tpu as pltpu
from jax.sharding import PartitionSpec as P

ROTS = 64
DEFOCI = 16
GRID = 7
NOISE_PRECISION = 4.0
AMPLITUDE = 0.07


def split_halves(table):
    rounded = lax.reduce_precision(table, 8, 7)
    high = rounded.astype(jnp.bfloat16)
    low = (table - rounded).astype(jnp.bfloat16)
    return jnp.concatenate([high, low], axis=0)


def contrast_table(band_value, plane_count, band_count):
    rows = jnp.arange(DEFOCI * 4, dtype=jnp.int32)[:, None]
    cell = jnp.arange(plane_count * plane_count, dtype=jnp.int32)[None, :]
    defocus = rows // 4
    real_x = (plane_count * (rows % 2) - plane_count + cell // plane_count).astype(jnp.float32)
    real_y = (plane_count * (rows // 2 % 2) - plane_count + cell % plane_count).astype(jnp.float32)
    radial = (real_x * real_x + real_y * real_y) / (2.0 * plane_count) ** 2 + (
        (band_value + 1.0) / band_count
    ) ** 2 / 4.0
    strength = 2.0 + 6.0 * defocus.astype(jnp.float32) / DEFOCI
    aberration = 8.0 * math.pi * strength * radial
    contrast = -(
        math.sqrt(1.0 - AMPLITUDE * AMPLITUDE) * jnp.sin(aberration)
        + AMPLITUDE * jnp.cos(aberration)
    )
    return split_halves(contrast)


def phase_table(plane_count, pad):
    steps = (jnp.arange(8, dtype=jnp.int32) - 3)[:, None]
    cell = jnp.arange(plane_count * plane_count, dtype=jnp.int32)[None, :]
    unit = 2.0 * math.pi / (4.0 * plane_count)
    along_x = unit * ((cell // plane_count) * steps).astype(jnp.float32)
    along_y = unit * ((cell % plane_count) * steps).astype(jnp.float32)
    cos_x, sin_x, cos_y, sin_y = lax.optimization_barrier(
        (jnp.cos(along_x), jnp.sin(along_x), jnp.cos(along_y[:GRID]), jnp.sin(along_y[:GRID]))
    )
    cosine = cos_y[:, None] * cos_x[None] - sin_y[:, None] * sin_x[None]
    sine = sin_y[:, None] * cos_x[None] + cos_y[:, None] * sin_x[None]
    both = [split_halves(t.reshape(GRID * 8, cell.shape[1])) for t in (cosine, sine)]
    both.append(jnp.zeros((pad - 4 * GRID * 8, cell.shape[1]), jnp.bfloat16))
    return jnp.concatenate(both, axis=0)


def selectors(shifts, defocus, tile_safe, pad):
    parity = tile_safe % 2 + 2 * (tile_safe // 2 % 2)
    pick = (
        (defocus * 4 + parity)[:, None]
        == (jnp.arange(2 * DEFOCI * 4, dtype=jnp.int32) % (DEFOCI * 4))[None, :]
    ).astype(jnp.bfloat16)
    sx = shifts % GRID - 3
    sy = shifts // GRID - 3
    quarter = ((1 - tile_safe % 2) * sx + (1 - tile_safe // 2 % 2) * sy + 64) % 4
    real_turn = jnp.where(quarter == 0, 1.0, jnp.where(quarter == 2, -1.0, 0.0))
    imag_turn = jnp.where(quarter == 1, -1.0, jnp.where(quarter == 3, 1.0, 0.0))
    column = jnp.arange(pad, dtype=jnp.int32)
    count = GRID * 8
    match = ((shifts + shifts // GRID)[:, None] == (column % count)[None, :]).astype(jnp.float32)
    is_cos = (column < 2 * count).astype(jnp.float32)[None, :]
    is_sin = ((column >= 2 * count) & (column < 4 * count)).astype(jnp.float32)[None, :]
    cosine = match * (real_turn[:, None] * is_cos - imag_turn[:, None] * is_sin)
    sine = match * (imag_turn[:, None] * is_cos + real_turn[:, None] * is_sin)
    return pick, cosine.astype(jnp.bfloat16), sine.astype(jnp.bfloat16)


def row_weights(rotation, bins, tile_safe, occupied, band_value, tile_count, plane_count):
    pose_angle = (
        2.0 * math.pi / ROTS * rotation.astype(jnp.float32)
        + 0.7 * bins.astype(jnp.float32)
        + 1.3 * tile_safe.astype(jnp.float32)
        + 0.5 * band_value
    )
    centre = 0.5 * (plane_count - 1) + 0.45 * plane_count * jnp.sin(pose_angle)
    column = jnp.arange(tile_count * plane_count, dtype=jnp.int32)
    plane = (column % plane_count).astype(jnp.float32)
    offset = (plane[None, :] - centre[:, None]) / 1.5
    weights = jnp.exp(-0.5 * offset * offset)
    mine = (tile_safe[:, None] == (column // plane_count)[None, :]) & (occupied > 0)[:, None]
    return jnp.where(mine, weights, 0.0).astype(jnp.bfloat16)


def fused_step(
    scale, bands, w_ref, wt_ref, pick_ref, cos_ref, sin_ref, ctf_ref, phase_ref, shard_ref, images_ref,
    out_ref, loss_ref,
    map_ref, mine, theirs, pair_in, chip_in, final,
    img_ref, img_sem, own_sem, map_send, map_recv, share_send, share_recv,
    pair_send, pair_recv, chip_send, chip_recv, band_send, band_recv,
):
    f32 = jnp.float32
    _, groups, depth, cols = map_ref.shape
    rounds = groups // 2
    chips = groups
    tiles, planes = out_ref.shape[1], depth // out_ref.shape[1]
    part = out_ref.shape[2]
    me = lax.axis_index("bins")
    chip, core = me // 2, me % 2
    band = lax.axis_index("shells")
    tile = min(256, cols)
    mesh_ids = pl.DeviceIdType.MESH

    rows = w_ref.shape[0]

    def fetch(lane):
        cells = pl.ds(pl.multiple_of(lane * 128, 128), 128)
        return pltpu.make_async_copy(
            images_ref.at[:, 0, :, cells], img_ref.at[lane], img_sem.at[lane]
        )

    def start_fetch(lane, carry):
        fetch(lane).start()
        return carry

    partner = {"bins": chip * 2 + (1 - core)}
    peers = [{"bins": (chip + r) % chips * 2 + core} for r in range(1, chips)]
    stack = [{"shells": (band + q) % bands} for q in range(1, bands)]
    barrier = pltpu.get_barrier_semaphore()
    for other in [partner] + peers + stack:
        pl.semaphore_signal(barrier, inc=1, device_id=other, device_id_type=mesh_ids)
    pl.semaphore_wait(barrier, 1 + len(peers) + len(stack))

    def block_of(device):
        return map_ref.at[device // groups, device % groups]

    def to_map(hop):
        return pltpu.make_async_remote_copy(
            src_ref=shard_ref, dst_ref=block_of(me),
            send_sem=map_send.at[hop - 1], recv_sem=map_recv.at[hop - 1],
            device_id=peers[hop - 1], device_id_type=mesh_ids,
        )

    def to_share(hop):
        source = (chip - hop + chips) % chips * 2 + core
        return pltpu.make_async_remote_copy(
            src_ref=block_of(source) if hop else shard_ref, dst_ref=block_of(source),
            send_sem=share_send.at[hop], recv_sem=share_recv.at[hop],
            device_id=partner, device_id_type=mesh_ids,
        )

    def hops_of(turn):
        return [(turn + 1) % chips, (turn + 1 + rounds) % chips]

    for turn in range(rounds):
        for hop in hops_of(turn):
            if hop:
                to_map(hop).start()
    to_share(0).start()
    keep = pltpu.make_async_copy(shard_ref, block_of(me), own_sem)
    keep.start()
    lax.fori_loop(0, img_ref.shape[0], start_fetch, 0)
    loss_ref[...] = jnp.zeros_like(loss_ref)

    def observed(start):
        lanes = []
        for at in range(tile // 128):
            lane = start // 128 + at
            fetch(lane).wait()
            lanes.append(img_ref[lane].reshape(rows, 128).astype(f32))
        return jnp.concatenate(lanes, axis=1)

    def compute(group, target):
        def columns(at, carry):
            inside = pl.ds(pl.multiple_of(at * tile, tile), tile)
            base = group * cols + at * tile
            cells = pl.ds(pl.multiple_of(base, tile), tile)
            weights = w_ref[...]
            phases = phase_ref[:, cells]
            part_a = jnp.dot(weights, map_ref[0, group, :, inside], preferred_element_type=f32)
            part_b = jnp.dot(weights, map_ref[1, group, :, inside], preferred_element_type=f32)
            contrast = jnp.dot(pick_ref[...], ctf_ref[:, cells], preferred_element_type=f32)
            cosine = contrast * jnp.dot(cos_ref[...], phases, preferred_element_type=f32)
            sine = contrast * jnp.dot(sin_ref[...], phases, preferred_element_type=f32)
            resid_real = cosine * part_a + sine * part_b - observed(base)
            resid_imag = cosine * part_b - sine * part_a - observed(groups * cols + base)
            square = resid_real * resid_real + resid_imag * resid_imag
            total = square[:, :128]
            for lane in range(128, tile, 128):
                total = total + square[:, lane : lane + 128]
            loss_ref[...] += total
            cosine = scale * cosine
            sine = scale * sine
            grad_real = (cosine * resid_real - sine * resid_imag).astype(jnp.bfloat16)
            grad_imag = (sine * resid_real + cosine * resid_imag).astype(jnp.bfloat16)
            back = wt_ref[...]
            target[0, :, inside] = jnp.dot(back, grad_real, preferred_element_type=f32)
            target[1, :, inside] = jnp.dot(back, grad_imag, preferred_element_type=f32)
            return carry

        lax.fori_loop(0, cols // tile, columns, 0)

    def to_partner(turn):
        return pltpu.make_async_remote_copy(
            src_ref=theirs.at[turn], dst_ref=pair_in.at[turn],
            send_sem=pair_send.at[turn], recv_sem=pair_recv.at[turn],
            device_id=partner, device_id_type=mesh_ids,
        )

    def rows_of(t):
        return pl.ds(t * planes, planes)

    def to_chip(turn, hop, t):
        half = (chip + hop) % chips // rounds
        return pltpu.make_async_remote_copy(
            src_ref=mine.at[turn, half, rows_of(t)], dst_ref=chip_in.at[hop - 1, rows_of(t)],
            send_sem=chip_send.at[hop - 1, t], recv_sem=chip_recv.at[hop - 1, t],
            device_id=peers[hop - 1], device_id_type=mesh_ids,
        )

    def to_band(hop, t):
        there = (band + hop) % bands
        return pltpu.make_async_remote_copy(
            src_ref=final.at[pl.ds(pl.multiple_of(t * planes + there * part, 8), part)],
            dst_ref=out_ref.at[band, t],
            send_sem=band_send.at[hop - 1, t], recv_sem=band_recv.at[hop - 1, t],
            device_id=stack[hop - 1], device_id_type=mesh_ids,
        )

    def combine(turn):
        to_partner(turn).wait_recv()
        for t in range(tiles):
            for half in range(2):
                mine[turn, half, rows_of(t)] += pair_in[turn, half, rows_of(t)]
            for hop in hops_of(turn):
                if hop:
                    to_chip(turn, hop, t).start()

    for turn in range(rounds):
        pair = (chip + turn + 1) % rounds
        for hop in hops_of(turn):
            if hop:
                to_map(chips - hop).wait_recv()
                to_share(chips - hop).start()
            else:
                keep.wait()
        compute(pair * 2 + core, mine.at[turn])
        if turn:
            combine(turn - 1)
        for hop in hops_of(turn):
            to_share((chips - hop) % chips).wait_recv()
        compute(pair * 2 + (1 - core), theirs.at[turn])
        to_partner(turn).start()
    combine(rounds - 1)

    own = chip // rounds
    for t in range(tiles):
        total = mine[rounds - 1, own, rows_of(t)]
        for hop in range(1, chips):
            to_chip((hop - 1) % rounds, hop, t).wait_recv()
            total = total + chip_in[hop - 1, rows_of(t)]
        final[rows_of(t)] = total
        for hop in range(1, bands):
            to_band(hop, t).start()
        out_ref[band, t] = final[pl.ds(pl.multiple_of(t * planes + band * part, 8), part)]

    to_share(0).wait_send()
    for hop in range(1, chips):
        to_map(hop).wait_send()
        to_share(hop).wait_send()
    for turn in range(rounds):
        to_partner(turn).wait_send()
    for t in range(tiles):
        for hop in range(1, chips):
            to_chip((hop - 1) % rounds, hop, t).wait_send()
        for hop in range(1, bands):
            to_band(hop, t).wait()


def local_step(scale, bands, tiles, weights, pick, cosine, sine, ctf, phase, shard, bins, images):
    rows, depth = weights.shape
    groups, cols = bins // 2, shard.shape[1]
    rounds, part = groups // 2, depth // tiles // bands
    f32 = jnp.float32
    lanes = images.shape[3] // 128
    vmem = pl.BlockSpec(memory_space=pltpu.VMEM)
    dma = pltpu.SemaphoreType.DMA
    return pl.pallas_call(
        lambda *refs: fused_step(scale, bands, *refs),
        in_specs=[vmem] * 8 + [pl.BlockSpec(memory_space=pl.ANY)],
        out_specs=[vmem] * 2,
        out_shape=[
            jax.ShapeDtypeStruct((bands, tiles, part, cols), f32),
            jax.ShapeDtypeStruct((rows, 128), f32),
        ],
        scratch_shapes=[
            pltpu.VMEM((2, groups, depth, cols), jnp.bfloat16),
            pltpu.VMEM((rounds, 2, depth, cols), f32),
            pltpu.VMEM((rounds, 2, depth, cols), f32),
            pltpu.VMEM((rounds, 2, depth, cols), f32),
            pltpu.VMEM((groups - 1, depth, cols), f32),
            pltpu.VMEM((depth, cols), f32),
            pltpu.VMEM((lanes, images.shape[0], images.shape[2], 128), jnp.bfloat16),
            dma((lanes,)),
            dma,
            dma((groups - 1,)),
            dma((groups - 1,)),
            dma((groups,)),
            dma((groups,)),
            dma((rounds,)),
            dma((rounds,)),
            dma((groups - 1, tiles)),
            dma((groups - 1, tiles)),
            dma((bands - 1, tiles)),
            dma((bands - 1, tiles)),
        ],
        compiler_params=pltpu.CompilerParams(
            vmem_limit_bytes=62 * 2**20, collective_id=0, has_side_effects=True
        ),
    )(weights, weights.T, pick, cosine, sine, ctf, phase, shard, images)


def on_device(map_tiles, images, pose_bin, rot_index, shift_index, defocus_class, tile_slots):
    band_index = lax.axis_index("shells")
    band_value = band_index.astype(jnp.float32)
    bin_count = lax.axis_size("bins")
    band_count = lax.axis_size("shells")
    part_count, _, slot_count, column_count = images.shape
    _, tile_count, plane_count, shard_cols = map_tiles.shape
    rows = part_count * slot_count
    depth = tile_count * plane_count
    grad_scale = NOISE_PRECISION / math.sqrt(part_count * bin_count)
    band_slots = lax.dynamic_index_in_dim(tile_slots, band_index, 1, keepdims=False)

    def per_row(values):
        return jnp.repeat(values, slot_count)

    bins = per_row(pose_bin[:, 0])
    slot = jnp.arange(rows, dtype=jnp.int32) % slot_count
    flat_slots = band_slots.reshape(-1)
    chosen = (bins * slot_count + slot)[:, None] == jnp.arange(flat_slots.shape[0])[None, :]
    tiles = jnp.sum(jnp.where(chosen, flat_slots[None, :], 0), axis=1)
    occupied = (tiles >= 0).astype(jnp.float32)
    tile_safe = jnp.maximum(tiles, 0)
    weights = row_weights(
        per_row(rot_index), bins, tile_safe, occupied, band_value, tile_count, plane_count
    )
    pad = 256
    pick, cosine, sine = selectors(per_row(shift_index), per_row(defocus_class), tile_safe, pad)
    ctf = contrast_table(band_value, plane_count, band_count)
    phase = phase_table(plane_count, pad)
    gradient, losses = local_step(
        grad_scale, band_count, tile_count, weights, pick, cosine, sine, ctf, phase,
        map_tiles.reshape(depth, shard_cols), bin_count, images,
    )
    band_loss = (
        2.0
        * jnp.sum((losses * occupied[:, None]).reshape(part_count, slot_count * 128), axis=1)
        / (slot_count * column_count)
    )
    return (gradient, band_loss[:, None])


def solution(mesh):
    return jax.shard_map(
        on_device,
        mesh=mesh,
        in_specs=(
            P("shells", None, None, "bins"),
            P("bins", "shells", None, None),
            P("bins", None),
            P("bins"),
            P("bins"),
            P("bins"),
            P(),
        ),
        out_specs=(P(None, None, "shells", "bins"), P("bins", "shells")),
        check_vma=False,
    )
```
